1024 devices in a mesh: wide: 64 (over x, y, core), narrow: 16 (over z).
Axes of the slice: x: 4, y: 8, z: 16, core: 2. Of those that a mesh axis runs over, the one named last changes fastest.
Arguments:
- amplitudes: bfloat16 [8192, 1024], P('narrow'), may hold values from -6 to 6
- integrals: bfloat16 [4096, 128, 128], P('wide', 'narrow'), may hold values from -0.5 to 0.5
- in_tile: int32 [4096], P('wide'), may hold values from 0 to 7
- counts: int32 [64], P('wide'), may hold values from 1 to 64, as said below
- out_tile: int32 [4096], P('wide'), may hold values from 0 to 127, as said below
- owner_map: int32 [128], replicated, may hold values from 0 to 127, as said below
Outputs:
- residual: float32 [8192, 16384], P('narrow', 'wide')
The draws below stay inside these ranges and needn't reach their ends.
Inputs may be any that keep to these rules, and one draw needn't show every extreme that they name: `counts`: some home device has exactly 64 live tasks in every draw. `out_tile`: call device owner_map[t] // 2 the owner of tile t. The 64 slots of one home device have tiles of pairwise different owners, and the live tasks of all homes give one owner at most 32 tasks; some owner receives exactly 32 in every draw. `owner_map`: A permutation of the residual tiles.
All inputs are finite; a program needn't handle non-finite values.
Results may differ from the reference program's by a relative error of at most 0.0029.
Values may be sent and summed in bfloat16 or wider, within the bound.
A program may use at most 32 MiB of HBM per device.

```python
import jax
import jax.numpy as jnp
from jax import lax

TILE = 128
KT = 8
OWN = 2
HOLD = 64
RECV = 32
ROWS = 8192
TASKS = 4096
NOUT = 128


def plan_draw(key):
    homes = TASKS // HOLD
    half = RECV
    owner_perm = jax.random.permutation(jax.random.fold_in(key, 101), NOUT).astype(jnp.int32)
    inverse = jnp.zeros((NOUT,), jnp.int32).at[owner_perm].set(jnp.arange(NOUT, dtype=jnp.int32))
    order = jax.random.permutation(jax.random.fold_in(key, 102), homes).astype(jnp.int32)
    first = order[:homes // 2]
    second = order[homes // 2:]
    spread = jax.random.randint(jax.random.fold_in(key, 103), (homes // 2,), 0, half - 1).astype(jnp.int32)
    first_counts = (half + spread).at[0].set(HOLD)
    second_counts = (half - 1 - spread).at[0].set(1)
    live_counts = jnp.zeros((homes,), jnp.int32).at[first].set(first_counts).at[second].set(second_counts)
    starts = jnp.cumsum(live_counts) - live_counts
    slot_ids = jnp.arange(HOLD, dtype=jnp.int32)[None, :]
    target = (starts[:, None] + slot_ids) % homes
    local_slot = jax.random.randint(jax.random.fold_in(key, 105), (homes, HOLD), 0, OWN).astype(jnp.int32)
    out_ids = inverse[target * OWN + local_slot].reshape(TASKS)
    return (live_counts, out_ids, owner_perm)


def draw_counts(key, part):
    return plan_draw(key)[0]


def draw_out_tile(key, part):
    return plan_draw(key)[1]


def draw_owner_map(key, part):
    return plan_draw(key)[2]


def with_ends(drawn, key, least, high):
    shape = drawn.shape
    spot = [jax.random.randint(jax.random.fold_in(key, axis), (), 0, shape[axis]) for axis in range(len(shape))]
    drawn = drawn.at[tuple(spot)].set(least)
    longest = shape.index(max(shape))
    spot[longest] = (spot[longest] + 1) % shape[longest]
    return drawn.at[tuple(spot)].set(high)


def levels(key, dims, cuts, smallest, top_value):
    def one(axis_at, blocks):
        steps = jax.random.uniform(jax.random.fold_in(jax.random.fold_in(key, 6), axis_at), (blocks,), jnp.float32, smallest / len(cuts), top_value / len(cuts))
        return jnp.repeat(jnp.exp(steps), dims[axis_at] // blocks).reshape((-1,) + (1,) * (len(dims) - axis_at - 1))

    gain = one(*cuts[0])
    for cut in cuts[1:]:
        gain = gain * one(*cut)
    return gain


def centred(key, shape, scale, reach, cuts=(), kind=jnp.bfloat16):
    array = jax.random.normal(key, shape, jnp.float32) * scale
    if len(cuts) > 0:
        array = levels(key, shape, cuts, -0.22, 0.18) * array
    return jnp.clip(array, min=-reach, max=reach).astype(kind)


def setup_inputs(seed: int = 0) -> dict:
    key_of = jax.random.split(jax.random.key(seed), 7)
    return {
        "amplitudes": centred(key_of[0], (ROWS, KT * TILE), 1.0, 6.0, ((0, 16),)),
        "integrals": centred(key_of[1], (TASKS, TILE, TILE), TILE ** -0.5, 0.5, ((0, 64), (1, 16))),
        "in_tile": with_ends(jax.random.randint(key_of[2], (TASKS,), 0, KT), jax.random.fold_in(key_of[2], 1), 0, KT - 1).astype(jnp.int32),
        "counts": draw_counts(jax.random.fold_in(key_of[6], 71), 0),
        "out_tile": draw_out_tile(jax.random.fold_in(key_of[6], 71), 0),
        "owner_map": draw_owner_map(jax.random.fold_in(key_of[6], 71), 0),
    }


def reference(amplitudes, integrals, in_tile, counts, out_tile, owner_map):
    amp_blocks = amplitudes.reshape(ROWS, KT, TILE)

    def add_task(running, task_index):
        is_live = (task_index % HOLD) < counts[task_index // HOLD]

        def compute(_):
            columns = lax.dynamic_index_in_dim(amp_blocks, in_tile[task_index].astype(jnp.int32), 1, keepdims=False)
            integral_tile = lax.dynamic_index_in_dim(integrals, task_index, 0, keepdims=False)
            product = jnp.dot(columns, integral_tile, preferred_element_type=jnp.float32).astype(jnp.bfloat16)
            product = lax.optimization_barrier(product)
            return product.astype(jnp.float32)

        def skipped(_):
            return jnp.zeros((ROWS, TILE), jnp.float32)

        product = lax.cond(is_live, compute, skipped, 0)
        place_at = owner_map[out_tile[task_index]].astype(jnp.int32)
        current = lax.dynamic_index_in_dim(running, place_at, 0, keepdims=False)
        running = lax.dynamic_update_index_in_dim(running, current + product, place_at, 0)
        return running, 0

    start_sum = jnp.zeros((NOUT, ROWS, TILE), jnp.float32)
    running, _ = lax.scan(add_task, start_sum, jnp.arange(TASKS, dtype=jnp.int32))
    return jnp.transpose(running, (1, 0, 2)).reshape(ROWS, NOUT * TILE)
```

```python
import jax
import jax.numpy as jnp
from jax import lax
from jax.sharding import PartitionSpec as P


def shards(amplitudes, integrals, in_tile, counts, out_tile, owner_map):
    slot_count, piece, width = integrals.shape
    tile_total = owner_map.shape[0]
    tile_count = amplitudes.shape[1] // width
    wide_count = lax.axis_size("wide")
    narrow_count = lax.axis_size("narrow")
    own_count = tile_total // wide_count
    bins = own_count * tile_count
    slot_ids = jnp.arange(slot_count, dtype=jnp.int32)
    is_live = slot_ids < counts[0]
    hit = out_tile[:, None] == jnp.arange(tile_total, dtype=jnp.int32)[None, :]
    place = jnp.sum(jnp.where(hit, owner_map[None, :], 0), axis=1)
    label = (place % own_count) * tile_count + in_tile + 1
    target = jnp.where(is_live, place // own_count, -1)
    owners = jnp.arange(wide_count, dtype=jnp.int32)[:, None]
    send_match = (target[None, :] == owners).astype(jnp.bfloat16)
    rows = jnp.concatenate(
        [
            integrals.reshape(slot_count, piece * width),
            jnp.broadcast_to(label[:, None], (slot_count, width)).astype(jnp.bfloat16),
        ],
        axis=1,
    )
    send = jnp.dot(send_match, rows, preferred_element_type=jnp.float32).astype(jnp.bfloat16)
    got = lax.all_to_all(send, "wide", split_axis=0, concat_axis=0, tiled=True)
    got_label = got[:, piece * width].astype(jnp.int32) - 1
    pick = (jnp.arange(bins, dtype=jnp.int32)[:, None] == got_label[None, :]).astype(jnp.bfloat16)
    summed = jnp.dot(
        pick, got[:, : piece * width], preferred_element_type=jnp.float32
    ).astype(jnp.bfloat16)
    summed = summed.reshape(own_count, tile_count, piece, width)
    full = lax.all_gather(summed, "narrow", axis=0)
    full = full.transpose(2, 0, 3, 1, 4)
    full = full.reshape(tile_count, narrow_count * piece, own_count * width)
    full = full.reshape(tile_count * narrow_count * piece, own_count * width)
    return jnp.dot(amplitudes, full, preferred_element_type=jnp.float32)


def solution(mesh):
    return jax.shard_map(
        shards,
        mesh=mesh,
        in_specs=(
            P("narrow", None),
            P("wide", "narrow", None),
            P("wide"),
            P("wide"),
            P("wide"),
            P(),
        ),
        out_specs=P("narrow", "wide"),
        check_vma=False,
    )
```

```python
import functools

import jax
import jax.numpy as jnp
from jax import lax
from jax.experimental import pallas as pl
from jax.experimental.pallas import tpu as pltpu
from jax.sharding import PartitionSpec as P

MESH = pl.DeviceIdType.MESH
CORES = 2
LABELS = 32


def far_first(count):
    return sorted(range(1, count), key=lambda d: -min(d, count - d))


def exchange(
    sizes,
    code_ref,
    tiles_ref,
    full_ref,
    send,
    send_label,
    mid,
    mid_label,
    got,
    got_label,
    y_send,
    y_recv,
    yl_send,
    yl_recv,
    e_send,
    e_recv,
    el_send,
    el_recv,
    up_send,
    up_recv,
    down_send,
    down_recv,
):
    x_count, y_count, own_count, tile_count = sizes
    e_count = x_count * CORES
    width = tiles_ref.shape[2]
    n_count = lax.axis_size("narrow")
    wide = lax.axis_index("wide")
    me = lax.axis_index("narrow")
    core = wide % CORES
    y = (wide // CORES) % y_count
    x = wide // (CORES * y_count)

    def wide_at(dy, de):
        to_x = (x + de // CORES) % x_count
        to_y = (y + dy) % y_count
        to_core = (core + de % CORES) % CORES
        return (to_x * y_count + to_y) * CORES + to_core

    up, down = (me + 1) % n_count, (me + n_count - 1) % n_count
    y_order = far_first(y_count)
    e_order = sorted(range(1, e_count), key=lambda d: -min(d // CORES, x_count - d // CORES))

    barrier = pltpu.get_barrier_semaphore()
    for dy in y_order:
        pl.semaphore_signal(barrier, inc=1, device_id={"wide": wide_at(dy, 0)}, device_id_type=MESH)
    for de in e_order:
        pl.semaphore_signal(barrier, inc=1, device_id={"wide": wide_at(0, de)}, device_id_type=MESH)
    pl.semaphore_signal(barrier, inc=1, device_id={"narrow": up}, device_id_type=MESH)
    pl.semaphore_signal(barrier, inc=1, device_id={"narrow": down}, device_id_type=MESH)

    for dy in y_order + [0]:
        rows, labels = (send.at[dy], send_label.at[dy]) if dy else (mid.at[0], mid_label.at[0])
        for de in range(e_count):
            code = code_ref[wide_at(dy, de)]
            rows[de] = tiles_ref[code // LABELS]
            labels[de] = jnp.full((1, width), code % LABELS, jnp.int32).astype(jnp.float32)

    pl.semaphore_wait(barrier, y_count + e_count)

    started = []

    def start(src, dst, send_sem, recv_sem, device):
        copy = pltpu.make_async_remote_copy(
            src_ref=src,
            dst_ref=dst,
            send_sem=send_sem,
            recv_sem=recv_sem,
            device_id=device,
            device_id_type=MESH,
        )
        copy.start()
        started.append(copy)
        return copy

    first = []
    for dy in y_order:
        to = {"wide": wide_at(dy, 0)}
        first.append(start(send_label.at[dy], mid_label.at[dy], yl_send.at[dy], yl_recv.at[dy], to))
        first.append(start(send.at[dy], mid.at[dy], y_send.at[dy], y_recv.at[dy], to))
    for copy in first:
        copy.wait_recv()
    second = {}
    for de in e_order:
        to = {"wide": wide_at(0, de)}
        second[de] = (
            start(mid_label.at[:, de], got_label.at[de], el_send.at[de], el_recv.at[de], to),
            start(mid.at[:, de], got.at[de], e_send.at[de], e_recv.at[de], to),
        )

    bins = own_count * tile_count
    sums = [jnp.zeros(tiles_ref.shape[1:], jnp.float32) for _ in range(bins)]
    for de in [0] + e_order[::-1]:
        for copy in second.get(de, ()):
            copy.wait_recv()
        for j in range(y_count):
            tile = (got[de, j] if de else mid[j, 0]).astype(jnp.float32)
            label = got_label[de, j] if de else mid_label[j, 0]
            label = jnp.broadcast_to(label, tile.shape)
            for b in range(bins):
                sums[b] = sums[b] + jnp.where(label == float(b + 1), tile, 0.0)
    for q in range(own_count):
        for k in range(tile_count):
            full_ref[k, me, :, q * width : (q + 1) * width] = sums[q * tile_count + k].astype(
                jnp.bfloat16
            )

    up_steps, down_steps = n_count // 2, (n_count - 1) // 2
    ups, downs = [], []
    for step in range(up_steps):
        if step:
            ups[-1].wait_recv()
        block = full_ref.at[:, (me + n_count - step) % n_count]
        ups.append(start(block, block, up_send.at[step], up_recv.at[step], {"narrow": up}))
        if step < down_steps:
            if step:
                downs[-1].wait_recv()
            block = full_ref.at[:, (me + step) % n_count]
            downs.append(
                start(block, block, down_send.at[step], down_recv.at[step], {"narrow": down})
            )
    ups[-1].wait_recv()
    if downs:
        downs[-1].wait_recv()
    for copy in started:
        copy.wait_send()


def shards(x_count, y_count, amplitudes, integrals, in_tile, counts, out_tile, owner_map):
    slot_count, piece, width = integrals.shape
    tile_total = owner_map.shape[0]
    wide_count = lax.axis_size("wide")
    narrow_count = lax.axis_size("narrow")
    tile_count = amplitudes.shape[1] // (piece * narrow_count)
    own_count = tile_total // wide_count
    e_count = x_count * CORES
    slot_ids = jnp.arange(slot_count, dtype=jnp.int32)
    hit = out_tile[:, None] == jnp.arange(tile_total, dtype=jnp.int32)[None, :]
    place = jnp.sum(jnp.where(hit, owner_map[None, :], 0), axis=1)
    label = (place % own_count) * tile_count + in_tile + 1
    target = jnp.where(slot_ids < counts[0], place // own_count, -1)
    owners = jnp.arange(wide_count, dtype=jnp.int32)[:, None]
    slot_code = slot_ids * LABELS + label
    code = jnp.sum(jnp.where(target[None, :] == owners, slot_code[None, :], 0), axis=1)
    rows = pltpu.VMEM
    dma = pltpu.SemaphoreType.DMA
    bf16, f32 = jnp.bfloat16, jnp.float32
    full = pl.pallas_call(
        functools.partial(exchange, (x_count, y_count, own_count, tile_count)),
        out_shape=jax.ShapeDtypeStruct((tile_count, narrow_count, piece, own_count * width), bf16),
        in_specs=[
            pl.BlockSpec(memory_space=pltpu.SMEM),
            pl.BlockSpec(memory_space=pltpu.VMEM),
        ],
        out_specs=pl.BlockSpec(memory_space=pltpu.VMEM),
        scratch_shapes=[
            rows((y_count, e_count, piece, width), bf16),
            rows((y_count, e_count, 1, width), f32),
            rows((y_count, e_count, piece, width), bf16),
            rows((y_count, e_count, 1, width), f32),
            rows((e_count, y_count, piece, width), bf16),
            rows((e_count, y_count, 1, width), f32),
        ]
        + [dma((y_count,))] * 4
        + [dma((e_count,))] * 4
        + [dma((narrow_count,))] * 4,
        compiler_params=pltpu.CompilerParams(collective_id=0, has_side_effects=True),
    )(code, integrals)
    full = full.reshape(tile_count * narrow_count * piece, own_count * width)
    return jnp.dot(amplitudes, full, preferred_element_type=jnp.float32)


def solution(mesh):
    wide_count = mesh.shape["wide"]
    y_count = 8 if wide_count == 64 else 2
    x_count = wide_count // (CORES * y_count)
    return jax.shard_map(
        functools.partial(shards, x_count, y_count),
        mesh=mesh,
        in_specs=(
            P("narrow", None),
            P("wide", "narrow", None),
            P("wide"),
            P("wide"),
            P("wide"),
            P(),
        ),
        out_specs=P("narrow", "wide"),
        check_vma=False,
    )
```

```python
import functools

import jax
import jax.numpy as jnp
from jax import lax
from jax.experimental import pallas as pl
from jax.experimental.pallas import tpu as pltpu
from jax.sharding import PartitionSpec as P

MESH = pl.DeviceIdType.MESH
CORES = 2
LABELS = 32
FANS = 4


def away(d, count):
    return min(d, count - d)


def exchange(
    sizes,
    tiles_hbm,
    in_hbm,
    counts_ref,
    out_hbm,
    map_hbm,
    full_ref,
    tiles_ref,
    in_ref,
    out_tile_ref,
    map_ref,
    code_vmem,
    code_ref,
    send,
    send_label,
    got,
    got_label,
    block_ref,
    load_sem,
    tile_send,
    tile_recv,
    label_send,
    label_recv,
    block_send,
    far_recv,
    near_recv,
):
    x_count, y_count, own_count, tile_count = sizes
    e_count = x_count * CORES
    wide_count = e_count * y_count
    slot_count, _, width = tiles_ref.shape
    n_count = lax.axis_size("narrow")
    wide = lax.axis_index("wide")
    me = lax.axis_index("narrow")
    core = wide % CORES
    y = (wide // CORES) % y_count
    x = wide // (CORES * y_count)

    def wide_at(dy, de):
        to_x = (x + de // CORES) % x_count
        to_y = (y + dy) % y_count
        to_core = (core + de % CORES) % CORES
        return (to_x * y_count + to_y) * CORES + to_core

    stride = n_count // FANS
    far = [stride * i for i in sorted(range(1, FANS), key=lambda i: -away(i, FANS))]
    near = [(d if away(d, stride) < stride / 2 else None) for d in range(1, stride)]
    near = [d if d is None or d < stride / 2 else d - stride for d in near]
    side = jnp.where(core == 0, stride // 2, n_count - stride // 2)

    def at(offset):
        return (me + n_count + offset) % n_count

    near = [at(side if d is None else d) for d in near]
    column = [at(d) for d in far] + near
    column += [at(-side)] if stride > 1 and stride % 2 == 0 else []
    partners = [(dy, de) for dy in range(y_count) for de in range(e_count) if (dy, de) != (0, 0)]
    partners.sort(key=lambda p: -(away(p[0], y_count) + away(p[1] // CORES, x_count)))

    loads = [
        pltpu.make_async_copy(src, dst, load_sem.at[i])
        for i, (src, dst) in enumerate(
            [
                (out_hbm, out_tile_ref),
                (map_hbm, map_ref),
                (in_hbm, in_ref),
                (tiles_hbm, tiles_ref),
            ]
        )
    ]
    for load in loads:
        load.start()
    barrier = pltpu.get_barrier_semaphore()
    for dy, de in partners:
        pl.semaphore_signal(
            barrier, inc=1, device_id={"wide": wide_at(dy, de)}, device_id_type=MESH
        )
    for n in column:
        pl.semaphore_signal(barrier, inc=1, device_id={"narrow": n}, device_id_type=MESH)
    for load in loads[:3]:
        load.wait()

    bf16, f32, i32 = jnp.bfloat16, jnp.float32, jnp.int32
    tile_total = map_ref.shape[1]
    hit = lax.broadcasted_iota(i32, (tile_total, slot_count), 0) == jnp.broadcast_to(
        out_tile_ref[...], (tile_total, slot_count)
    )
    place = jnp.dot(
        jnp.broadcast_to(map_ref[...].astype(f32), (8, tile_total)).astype(bf16),
        hit.astype(f32).astype(bf16),
        preferred_element_type=f32,
    ).astype(i32)
    slot = lax.broadcasted_iota(i32, (8, slot_count), 1)
    target = jnp.where(slot < counts_ref[0], place // own_count, -1)
    label = (place % own_count) * tile_count + in_ref[...] + 1
    kinds = jnp.where(lax.broadcasted_iota(i32, (8, slot_count), 0) == 0, slot, label)
    match = lax.broadcasted_iota(i32, (wide_count, slot_count), 0) == jnp.broadcast_to(
        target[:1], (wide_count, slot_count)
    )
    found = lax.dot_general(
        kinds.astype(f32).astype(bf16),
        match.astype(f32).astype(bf16),
        (((1,), (1,)), ((), ())),
        preferred_element_type=f32,
    ).astype(i32)
    code_vmem[...] = found[:1] * LABELS + found[1:2]
    to_scalar = pltpu.make_async_copy(code_vmem, code_ref, load_sem.at[0])
    to_scalar.start()
    loads[3].wait()
    to_scalar.wait()

    for dy, de in partners + [(0, 0)]:
        spot = dy * e_count + de
        code = code_ref[0, wide_at(dy, de)]
        rows, labels = (send, send_label) if spot else (got, got_label)
        rows[spot] = tiles_ref[jnp.clip(code // LABELS, 0, slot_count - 1)]
        labels[spot] = jnp.full((1, width), code % LABELS, i32).astype(f32)

    pl.semaphore_wait(barrier, wide_count - 1 + len(column))

    def remote(src, dst, send_sem, recv_sem, device):
        return pltpu.make_async_remote_copy(
            src_ref=src,
            dst_ref=dst,
            send_sem=send_sem,
            recv_sem=recv_sem,
            device_id=device,
            device_id_type=MESH,
        )

    half = wide_count // 2
    for dy, de in partners:
        to = {"wide": wide_at(dy, de)}
        spot = dy * e_count + de
        group = spot // half
        remote(
            send_label.at[spot], got_label.at[spot], label_send, label_recv.at[group], to
        ).start()
        remote(send.at[spot], got.at[spot], tile_send, tile_recv.at[group], to).start()

    bins = own_count * tile_count
    sums = [jnp.zeros(tiles_ref.shape[1:], f32) for _ in range(bins)]
    to = {"wide": wide_at(0, 1)}
    for group in range(2):
        first = max(group * half, 1)
        part = pl.ds(first, (group + 1) * half - first)
        remote(send.at[part], got.at[part], tile_send, tile_recv.at[group], to).wait_recv()
        remote(
            send_label.at[part], got_label.at[part], label_send, label_recv.at[group], to
        ).wait_recv()
        for spot in range(group * half, (group + 1) * half):
            tile = got[spot].astype(f32)
            mark = jnp.broadcast_to(got_label[spot], tile.shape)
            for b in range(bins):
                sums[b] = sums[b] + jnp.where(mark == float(b + 1), tile, 0.0)
    for q in range(own_count):
        for k in range(tile_count):
            block_ref[k, :, q * width : (q + 1) * width] = sums[q * tile_count + k].astype(bf16)

    def pass_on(block, n, recv_sem, to):
        remote(block, full_ref.at[:, n], block_send, recv_sem, {"narrow": to}).start()

    for i, d in enumerate(far):
        pass_on(block_ref, me, far_recv.at[i], at(d))
    for n in near:
        pass_on(block_ref, me, near_recv, n)
    own_copy = pltpu.make_async_copy(block_ref, full_ref.at[:, me], load_sem.at[0])
    own_copy.start()
    for i, d in sorted(enumerate(far), key=lambda f: away(f[1], n_count)):
        n = at(-d)
        landed = full_ref.at[:, n]
        remote(block_ref, landed, block_send, far_recv.at[i], {"narrow": at(d)}).wait_recv()
        for to in near:
            pass_on(landed, n, near_recv, to)
    own_copy.wait()
    sent = full_ref.at[:, pl.ds(0, n_count - 1)]
    if near:
        landed = full_ref.at[:, pl.ds(0, FANS * len(near))]
        remote(landed, landed, block_send, near_recv, {"narrow": column[0]}).wait_recv()
    remote(sent, sent, block_send, near_recv, {"narrow": column[0]}).wait_send()
    every = pl.ds(1, wide_count - 1)
    remote(send.at[every], got.at[every], tile_send, tile_recv.at[0], to).wait_send()
    remote(
        send_label.at[every], got_label.at[every], label_send, label_recv.at[0], to
    ).wait_send()


def multiply(a_ref, b_ref, o_hbm, o_ref, sem):
    rows = a_ref.shape[0]
    step = min(128, rows)
    copies = []
    for i in range(rows // step):
        part = pl.ds(i * step, step)
        o_ref[part, :] = jnp.dot(a_ref[part, :], b_ref[...], preferred_element_type=jnp.float32)
        copies.append(pltpu.make_async_copy(o_ref.at[part], o_hbm.at[part], sem.at[i]))
        copies[-1].start()
    for copy in copies:
        copy.wait()


def pinned(operand):
    return pltpu.with_memory_space_constraint(operand, pltpu.HBM)


def shards(x_count, y_count, amplitudes, integrals, in_tile, counts, out_tile, owner_map):
    slot_count, piece, width = integrals.shape
    row_count, deep = amplitudes.shape
    tile_total = owner_map.shape[0]
    wide_count = lax.axis_size("wide")
    narrow_count = lax.axis_size("narrow")
    tile_count = deep // (piece * narrow_count)
    own_count = tile_total // wide_count
    wide_out = own_count * width
    vmem = pltpu.VMEM
    dma = pltpu.SemaphoreType.DMA
    bf16, f32, i32 = jnp.bfloat16, jnp.float32, jnp.int32
    hbm = pl.BlockSpec(memory_space=pl.ANY)
    whole = pl.BlockSpec(memory_space=pltpu.VMEM)
    full = pl.pallas_call(
        functools.partial(exchange, (x_count, y_count, own_count, tile_count)),
        out_shape=jax.ShapeDtypeStruct((tile_count, narrow_count, piece, wide_out), bf16),
        in_specs=[hbm, hbm, pl.BlockSpec(memory_space=pltpu.SMEM), hbm, hbm],
        out_specs=hbm,
        cost_estimate=pl.CostEstimate(flops=10**9, bytes_accessed=10**8, transcendentals=0),
        scratch_shapes=[
            vmem((slot_count, piece, width), bf16),
            vmem((1, slot_count), i32),
            vmem((1, slot_count), i32),
            vmem((1, tile_total), i32),
            vmem((1, wide_count), i32),
            pltpu.SMEM((1, wide_count), i32),
            vmem((wide_count, piece, width), bf16),
            vmem((wide_count, 1, width), f32),
            vmem((wide_count, piece, width), bf16),
            vmem((wide_count, 1, width), f32),
            vmem((tile_count, piece, wide_out), bf16),
            dma((4,)),
            dma(()),
            dma((2,)),
            dma(()),
            dma((2,)),
            dma(()),
            dma((FANS - 1,)),
            dma(()),
        ],
        compiler_params=pltpu.CompilerParams(
            collective_id=0, has_side_effects=True, vmem_limit_bytes=8 << 20
        ),
    )(
        pinned(integrals),
        pinned(in_tile.reshape(1, slot_count)),
        counts,
        pinned(out_tile.reshape(1, slot_count)),
        pinned(owner_map.reshape(1, tile_total)),
    )
    full = full.reshape(deep, wide_out)
    return pl.pallas_call(
        multiply,
        out_shape=jax.ShapeDtypeStruct((row_count, wide_out), f32),
        in_specs=[whole, whole],
        out_specs=hbm,
        scratch_shapes=[vmem((row_count, wide_out), f32), dma((8,))],
        compiler_params=pltpu.CompilerParams(vmem_limit_bytes=8 << 20),
    )(amplitudes, full)


def solution(mesh):
    wide_count = mesh.shape["wide"]
    y_count = 8 if wide_count == 64 else max(1, wide_count // 4)
    x_count = wide_count // (CORES * y_count)
    return jax.shard_map(
        functools.partial(shards, x_count, y_count),
        mesh=mesh,
        in_specs=(
            P("narrow", None),
            P("wide", "narrow", None),
            P("wide"),
            P("wide"),
            P("wide"),
            P(),
        ),
        out_specs=P("narrow", "wide"),
        check_vma=False,
    )
```

```python
import functools

import jax
import jax.numpy as jnp
from jax import lax
from jax.experimental import pallas as pl
from jax.experimental.pallas import tpu as pltpu
from jax.sharding import PartitionSpec as P

MESH = pl.DeviceIdType.MESH
CORES = 2
LABELS = 32
FANS = 4


def away(d, count):
    return min(d, count - d)


def exchange(
    sizes,
    tiles_hbm,
    in_hbm,
    counts_ref,
    out_hbm,
    map_hbm,
    full_ref,
    tiles_ref,
    in_ref,
    out_tile_ref,
    map_ref,
    code_vmem,
    code_ref,
    send,
    send_label,
    got,
    got_label,
    block_ref,
    load_sem,
    tile_send,
    tile_recv,
    label_send,
    label_recv,
    block_send,
    far_recv,
    half_recv,
    near_recv,
    plane_ready,
):
    x_count, y_count, own_count, tile_count = sizes
    chips = x_count * y_count
    wide_count = chips * CORES
    slot_count, _, width = tiles_ref.shape
    n_count = lax.axis_size("narrow")
    wide = lax.axis_index("wide")
    me = lax.axis_index("narrow")
    core = wide % CORES
    y = (wide // CORES) % y_count
    x = wide // (CORES * y_count)

    def wide_at(j, to_core):
        to_x = (x + j % x_count) % x_count
        to_y = (y + j // x_count) % y_count
        return (to_x * y_count + to_y) * CORES + to_core

    def at(offset):
        return (me + n_count + offset) % n_count

    stride = n_count // FANS
    side = jnp.where(core == 0, stride // 2, -(stride // 2))
    steps = [stride] + list(range(1, (stride + 1) // 2)) + ([side] if stride % 2 == 0 else [])
    column = [at(sign * d) for d in steps for sign in (1, -1)]
    near = list(range(2, 2 * len(steps)))[: stride - 1]
    order = sorted(
        range(chips), key=lambda j: -(away(j // x_count, y_count) + away(j % x_count, x_count))
    )
    others = [j for j in order if j]

    def signal(sem, device):
        pl.semaphore_signal(sem, inc=1, device_id=device, device_id_type=MESH)

    def remote(src, dst, send_sem, recv_sem, device):
        return pltpu.make_async_remote_copy(
            src_ref=src,
            dst_ref=dst,
            send_sem=send_sem,
            recv_sem=recv_sem,
            device_id=device,
            device_id_type=MESH,
        )

    loads = [
        pltpu.make_async_copy(src, dst, load_sem.at[i])
        for i, (src, dst) in enumerate(
            [(out_hbm, out_tile_ref), (map_hbm, map_ref), (in_hbm, in_ref), (tiles_hbm, tiles_ref)]
        )
    ]
    for load in loads:
        load.start()

    barrier = pltpu.get_barrier_semaphore()
    for j in order:
        signal(barrier, {"wide": wide_at(j, 1 - core)})
        if j:
            signal(barrier, {"wide": wide_at(j, core)})

    for n in column:

        @pl.when(n > me)
        def _(n=n):
            signal(barrier, {"narrow": n})

    for load in loads[:3]:
        load.wait()

    bf16, f32, i32 = jnp.bfloat16, jnp.float32, jnp.int32
    tile_total = map_ref.shape[1]
    hit = lax.broadcasted_iota(i32, (tile_total, slot_count), 0) == jnp.broadcast_to(
        out_tile_ref[...], (tile_total, slot_count)
    )
    place = jnp.dot(
        jnp.broadcast_to(map_ref[...].astype(f32), (8, tile_total)).astype(bf16),
        hit.astype(f32).astype(bf16),
        preferred_element_type=f32,
    ).astype(i32)
    slot = lax.broadcasted_iota(i32, (8, slot_count), 1)
    target = jnp.where(slot < counts_ref[0], place // own_count, -1)
    label = (place % own_count) * tile_count + in_ref[...] + 1
    kinds = jnp.where(lax.broadcasted_iota(i32, (8, slot_count), 0) == 0, slot, label)
    match = lax.broadcasted_iota(i32, (wide_count, slot_count), 0) == jnp.broadcast_to(
        target[:1], (wide_count, slot_count)
    )
    found = lax.dot_general(
        kinds.astype(f32).astype(bf16),
        match.astype(f32).astype(bf16),
        (((1,), (1,)), ((), ())),
        preferred_element_type=f32,
    ).astype(i32)
    code_vmem[...] = found[:1] * LABELS + found[1:2]
    to_scalar = pltpu.make_async_copy(code_vmem, code_ref, load_sem.at[0])
    to_scalar.start()
    loads[3].wait()
    to_scalar.wait()

    def gather(j, to_core, rows, labels, spot):
        code = code_ref[0, wide_at(j, to_core)]
        rows[spot] = tiles_ref[jnp.clip(code // LABELS, 0, slot_count - 1)]
        labels[spot] = jnp.full((1, width), code % LABELS, i32).astype(f32)

    for to_core in range(CORES):
        for j in order:
            gather(j, to_core, send, send_label, to_core * chips + j)
    gather(0, core, got, got_label, core * chips)

    lower = sum(jnp.where(n < me, 1, 0) for n in column)
    pl.semaphore_wait(barrier, wide_count - 1 + lower)

    def send_to(j, to_core):
        device = {"wide": wide_at(j, to_core)}
        out, spot, other = to_core * chips + j, core * chips + j, (core + to_core) % CORES
        remote(
            send_label.at[out], got_label.at[spot], label_send, label_recv.at[other], device
        ).start()
        remote(send.at[out], got.at[spot], tile_send, tile_recv.at[other], device).start()

    for j in others:
        for to_core in range(CORES):
            send_to(j, to_core)
    send_to(0, 1 - core)

    for i, n in enumerate(column):

        @pl.when(n < me)
        def _(i=i, n=n):
            signal(plane_ready.at[i ^ 1], {"narrow": n})

    bins = own_count * tile_count
    sums = [jnp.zeros(tiles_ref.shape[1:], f32) for _ in range(bins)]
    mate = {"wide": wide_at(0, 1 - core)}
    for other in range(CORES):
        base = (core if other == 0 else 1 - core) * chips
        part = pl.ds(base + 1, chips - 1) if other == 0 else pl.ds(base, chips)
        remote(got.at[part], got.at[part], tile_send, tile_recv.at[other], mate).wait_recv()
        remote(
            got_label.at[part], got_label.at[part], label_send, label_recv.at[other], mate
        ).wait_recv()
        for j in range(chips):
            tile = got[base + j].astype(f32)
            mark = jnp.broadcast_to(got_label[base + j], tile.shape)
            for b in range(bins):
                sums[b] = sums[b] + jnp.where(mark == float(b + 1), tile, 0.0)
    for q in range(own_count):
        for k in range(tile_count):
            block_ref[k, :, q * width : (q + 1) * width] = sums[q * tile_count + k].astype(bf16)

    def pass_on(src, dst, recv_sem, n):
        remote(src, dst, block_send, recv_sem, {"narrow": n}).start()

    def wait_ready(i, n):
        @pl.when(n > me)
        def _():
            pl.semaphore_wait(plane_ready.at[i], 1)

    mine = full_ref.at[:, me]
    first = jnp.where(column[0] < n_count // 2, 0, 1)
    sides = [
        (i, jnp.where(i == 0, column[0], column[1]), jnp.where(i == 0, column[1], column[0]))
        for i in (first, 1 - first)
    ]
    for i, n, _ in sides:
        wait_ready(i, n)
        pass_on(block_ref, mine, far_recv.at[1 - i], n)
    for i in near:
        wait_ready(i, column[i])
        pass_on(block_ref, mine, near_recv, column[i])
    for i in range(2 + len(near), len(column)):
        wait_ready(i, column[i])
    own_copy = pltpu.make_async_copy(block_ref, mine, load_sem.at[0])
    own_copy.start()
    size = tile_count // 2
    for i, n, beyond in sides:
        landed = full_ref.at[:, n]
        remote(landed, landed, block_send, far_recv.at[i], {"narrow": n}).wait_recv()
        half = full_ref.at[pl.ds((1 - i) * size, size), n]
        pass_on(half, half, half_recv.at[i], beyond)
        for to in near:
            pass_on(landed, landed, near_recv, column[to])
    for i, n, _ in sides:
        half = full_ref.at[pl.ds((1 - i) * size, size), at(n_count // 2)]
        remote(half, half, block_send, half_recv.at[i], {"narrow": n}).wait_recv()
        for to in near:
            pass_on(half, half, near_recv, column[to])
    own_copy.wait()
    if near:
        landed = full_ref.at[:, pl.ds(0, FANS * len(near))]
        remote(landed, landed, block_send, near_recv, {"narrow": column[0]}).wait_recv()
    sent = full_ref.at[:, pl.ds(0, n_count - 1)]
    remote(sent, sent, block_send, near_recv, {"narrow": column[0]}).wait_send()
    every = pl.ds(1, wide_count - 1)
    remote(send.at[every], got.at[every], tile_send, tile_recv.at[0], mate).wait_send()
    remote(
        send_label.at[every], got_label.at[every], label_send, label_recv.at[0], mate
    ).wait_send()


def multiply(a_ref, b_ref, o_hbm, o_ref, sem):
    rows = a_ref.shape[0]
    step = min(128, rows)
    copies = []
    for i in range(rows // step):
        part = pl.ds(i * step, step)
        o_ref[part, :] = jnp.dot(a_ref[part, :], b_ref[...], preferred_element_type=jnp.float32)
        copies.append(pltpu.make_async_copy(o_ref.at[part], o_hbm.at[part], sem.at[i]))
        copies[-1].start()
    for copy in copies:
        copy.wait()


def pinned(operand):
    return pltpu.with_memory_space_constraint(operand, pltpu.HBM)


def shards(x_count, y_count, amplitudes, integrals, in_tile, counts, out_tile, owner_map):
    slot_count, piece, width = integrals.shape
    row_count, deep = amplitudes.shape
    tile_total = owner_map.shape[0]
    wide_count = lax.axis_size("wide")
    narrow_count = lax.axis_size("narrow")
    tile_count = deep // (piece * narrow_count)
    own_count = tile_total // wide_count
    wide_out = own_count * width
    vmem = pltpu.VMEM
    dma = pltpu.SemaphoreType.DMA
    bf16, f32, i32 = jnp.bfloat16, jnp.float32, jnp.int32
    hbm = pl.BlockSpec(memory_space=pl.ANY)
    whole = pl.BlockSpec(memory_space=pltpu.VMEM)
    full = pl.pallas_call(
        functools.partial(exchange, (x_count, y_count, own_count, tile_count)),
        out_shape=jax.ShapeDtypeStruct((tile_count, narrow_count, piece, wide_out), bf16),
        in_specs=[hbm, hbm, pl.BlockSpec(memory_space=pltpu.SMEM), hbm, hbm],
        out_specs=hbm,
        cost_estimate=pl.CostEstimate(flops=10**9, bytes_accessed=10**8, transcendentals=0),
        scratch_shapes=[
            vmem((slot_count, piece, width), bf16),
            vmem((1, slot_count), i32),
            vmem((1, slot_count), i32),
            vmem((1, tile_total), i32),
            vmem((1, wide_count), i32),
            pltpu.SMEM((1, wide_count), i32),
            vmem((wide_count, piece, width), bf16),
            vmem((wide_count, 1, width), f32),
            vmem((wide_count, piece, width), bf16),
            vmem((wide_count, 1, width), f32),
            vmem((tile_count, piece, wide_out), bf16),
            dma((4,)),
            dma(()),
            dma((2,)),
            dma(()),
            dma((2,)),
            dma(()),
            dma((2,)),
            dma((2,)),
            dma(()),
            pltpu.SemaphoreType.REGULAR((narrow_count,)),
        ],
        compiler_params=pltpu.CompilerParams(
            collective_id=0, has_side_effects=True, vmem_limit_bytes=8 << 20
        ),
    )(
        pinned(integrals),
        pinned(in_tile.reshape(1, slot_count)),
        counts,
        pinned(out_tile.reshape(1, slot_count)),
        pinned(owner_map.reshape(1, tile_total)),
    )
    full = full.reshape(deep, wide_out)
    return pl.pallas_call(
        multiply,
        out_shape=jax.ShapeDtypeStruct((row_count, wide_out), f32),
        in_specs=[whole, whole],
        out_specs=hbm,
        scratch_shapes=[vmem((row_count, wide_out), f32), dma((8,))],
        compiler_params=pltpu.CompilerParams(vmem_limit_bytes=8 << 20),
    )(amplitudes, full)


def solution(mesh):
    wide_count = mesh.shape["wide"]
    y_count = 8 if wide_count == 64 else max(1, wide_count // 4)
    x_count = wide_count // (CORES * y_count)
    return jax.shard_map(
        functools.partial(shards, x_count, y_count),
        mesh=mesh,
        in_specs=(
            P("narrow", None),
            P("wide", "narrow", None),
            P("wide"),
            P("wide"),
            P("wide"),
            P(),
        ),
        out_specs=P("narrow", "wide"),
        check_vma=False,
    )
```

```python
import functools

import jax
import jax.numpy as jnp
from jax import lax
from jax.experimental import pallas as pl
from jax.experimental.pallas import tpu as pltpu
from jax.sharding import PartitionSpec as P

MESH = pl.DeviceIdType.MESH
CORES = 2
LABELS = 32
FANS = 4


def away(d, count):
    return min(d, count - d)


def exchange(
    sizes,
    tiles_hbm,
    in_hbm,
    counts_ref,
    out_hbm,
    map_hbm,
    full_ref,
    tiles_ref,
    in_ref,
    out_tile_ref,
    map_ref,
    code_vmem,
    code_ref,
    send,
    send_label,
    got,
    got_label,
    block_ref,
    load_sem,
    tile_send,
    tile_recv,
    label_send,
    label_recv,
    block_send,
    far_recv,
    half_recv,
    near_recv,
    plane_ready,
):
    x_count, y_count, own_count, tile_count = sizes
    chips = x_count * y_count
    wide_count = chips * CORES
    slot_count, _, width = tiles_ref.shape
    n_count = lax.axis_size("narrow")
    wide = lax.axis_index("wide")
    me = lax.axis_index("narrow")
    core = wide % CORES
    y = (wide // CORES) % y_count
    x = wide // (CORES * y_count)

    def wide_at(j, to_core):
        to_x = (x + j % x_count) % x_count
        to_y = (y + j // x_count) % y_count
        return (to_x * y_count + to_y) * CORES + to_core

    def at(offset):
        return (me + n_count + offset) % n_count

    stride = n_count // FANS
    side = jnp.where(core == 0, stride // 2, -(stride // 2))
    steps = [stride] + list(range(1, (stride + 1) // 2)) + ([side] if stride % 2 == 0 else [])
    column = [at(sign * d) for d in steps for sign in (1, -1)]
    near = list(range(2, 2 * len(steps)))[: stride - 1]
    order = sorted(
        range(chips), key=lambda j: -(away(j // x_count, y_count) + away(j % x_count, x_count))
    )
    others = [j for j in order if j]

    def signal(sem, device):
        pl.semaphore_signal(sem, inc=1, device_id=device, device_id_type=MESH)

    def remote(src, dst, send_sem, recv_sem, device):
        return pltpu.make_async_remote_copy(
            src_ref=src,
            dst_ref=dst,
            send_sem=send_sem,
            recv_sem=recv_sem,
            device_id=device,
            device_id_type=MESH,
        )

    loads = [
        pltpu.make_async_copy(src, dst, load_sem.at[i])
        for i, (src, dst) in enumerate(
            [(out_hbm, out_tile_ref), (map_hbm, map_ref), (in_hbm, in_ref), (tiles_hbm, tiles_ref)]
        )
    ]
    for load in loads:
        load.start()

    barrier = pltpu.get_barrier_semaphore()
    for j in order:
        signal(barrier, {"wide": wide_at(j, 1 - core)})
        if j:
            signal(barrier, {"wide": wide_at(j, core)})

    for n in column:

        @pl.when(n > me)
        def _(n=n):
            signal(barrier, {"narrow": n})

    for load in loads[:3]:
        load.wait()

    bf16, f32, i32 = jnp.bfloat16, jnp.float32, jnp.int32
    tile_total = map_ref.shape[1]
    hit = lax.broadcasted_iota(i32, (tile_total, slot_count), 0) == jnp.broadcast_to(
        out_tile_ref[...], (tile_total, slot_count)
    )
    place = jnp.dot(
        jnp.broadcast_to(map_ref[...].astype(f32), (8, tile_total)).astype(bf16),
        hit.astype(f32).astype(bf16),
        preferred_element_type=f32,
    ).astype(i32)
    slot = lax.broadcasted_iota(i32, (8, slot_count), 1)
    target = jnp.where(slot < counts_ref[0], place // own_count, -1)
    label = (place % own_count) * tile_count + in_ref[...] + 1
    kinds = jnp.where(lax.broadcasted_iota(i32, (8, slot_count), 0) == 0, slot, label)
    match = lax.broadcasted_iota(i32, (wide_count, slot_count), 0) == jnp.broadcast_to(
        target[:1], (wide_count, slot_count)
    )
    found = lax.dot_general(
        kinds.astype(f32).astype(bf16),
        match.astype(f32).astype(bf16),
        (((1,), (1,)), ((), ())),
        preferred_element_type=f32,
    ).astype(i32)
    code_vmem[...] = found[:1] * LABELS + found[1:2]
    to_scalar = pltpu.make_async_copy(code_vmem, code_ref, load_sem.at[0])
    to_scalar.start()
    loads[3].wait()
    to_scalar.wait()

    def gather(j, to_core, rows, labels, spot):
        code = code_ref[0, wide_at(j, to_core)]
        rows[spot] = tiles_ref[jnp.clip(code // LABELS, 0, slot_count - 1)]
        labels[spot] = jnp.full((1, width), code % LABELS, i32).astype(f32)

    for to_core in range(CORES):
        for j in order:
            gather(j, to_core, send, send_label, to_core * chips + j)
    gather(0, core, got, got_label, core * chips)

    lower = sum(jnp.where(n < me, 1, 0) for n in column)
    pl.semaphore_wait(barrier, wide_count - 1 + lower)

    targets = [(j, to_core) for j in others for to_core in range(CORES)] + [(0, 1 - core)]
    for src, dst, s_sem, r_sem in (
        (send, got, tile_send, tile_recv),
        (send_label, got_label, label_send, label_recv),
    ):
        for j, to_core in targets:
            out, spot, other = to_core * chips + j, core * chips + j, (core + to_core) % CORES
            device = {"wide": wide_at(j, to_core)}
            remote(src.at[out], dst.at[spot], s_sem, r_sem.at[other], device).start()

    for i, n in enumerate(column):

        @pl.when(n < me)
        def _(i=i, n=n):
            signal(plane_ready.at[i ^ 1], {"narrow": n})

    bins = own_count * tile_count
    sums = [jnp.zeros(tiles_ref.shape[1:], f32) for _ in range(bins)]
    mate = {"wide": wide_at(0, 1 - core)}
    for other in range(CORES):
        base = (core if other == 0 else 1 - core) * chips
        part = pl.ds(base + 1, chips - 1) if other == 0 else pl.ds(base, chips)
        remote(got.at[part], got.at[part], tile_send, tile_recv.at[other], mate).wait_recv()
        remote(
            got_label.at[part], got_label.at[part], label_send, label_recv.at[other], mate
        ).wait_recv()
        for j in range(chips):
            tile = got[base + j].astype(f32)
            mark = jnp.broadcast_to(got_label[base + j], tile.shape)
            for b in range(bins):
                sums[b] = sums[b] + jnp.where(mark == float(b + 1), tile, 0.0)
    for q in range(own_count):
        for k in range(tile_count):
            block_ref[k, :, q * width : (q + 1) * width] = sums[q * tile_count + k].astype(bf16)

    def pass_on(src, dst, recv_sem, n):
        remote(src, dst, block_send, recv_sem, {"narrow": n}).start()

    def wait_ready(i, n):
        @pl.when(n > me)
        def _():
            pl.semaphore_wait(plane_ready.at[i], 1)

    mine = full_ref.at[:, me]
    first = jnp.where(column[0] < n_count // 2, 0, 1)
    sides = [
        (i, jnp.where(i == 0, column[0], column[1]), jnp.where(i == 0, column[1], column[0]))
        for i in (first, 1 - first)
    ]
    for i, n, _ in sides:
        wait_ready(i, n)
        pass_on(block_ref, mine, far_recv.at[1 - i], n)
    for i in near:
        wait_ready(i, column[i])
        pass_on(block_ref, mine, near_recv, column[i])
    for i in range(2 + len(near), len(column)):
        wait_ready(i, column[i])
    own_copy = pltpu.make_async_copy(block_ref, mine, load_sem.at[0])
    own_copy.start()
    size = tile_count // 2
    for i, n, beyond in sides:
        landed = full_ref.at[:, n]
        remote(landed, landed, block_send, far_recv.at[i], {"narrow": n}).wait_recv()
        half = full_ref.at[pl.ds((1 - i) * size, size), n]
        pass_on(half, half, half_recv.at[i], beyond)
        for to in near:
            pass_on(landed, landed, near_recv, column[to])
    for i, n, _ in sides:
        half = full_ref.at[pl.ds((1 - i) * size, size), at(n_count // 2)]
        remote(half, half, block_send, half_recv.at[i], {"narrow": n}).wait_recv()
        for to in near:
            pass_on(half, half, near_recv, column[to])
    own_copy.wait()
    if near:
        landed = full_ref.at[:, pl.ds(0, FANS * len(near))]
        remote(landed, landed, block_send, near_recv, {"narrow": column[0]}).wait_recv()
    sent = full_ref.at[:, pl.ds(0, n_count - 1)]
    remote(sent, sent, block_send, near_recv, {"narrow": column[0]}).wait_send()
    every = pl.ds(1, wide_count - 1)
    remote(send.at[every], got.at[every], tile_send, tile_recv.at[0], mate).wait_send()
    remote(
        send_label.at[every], got_label.at[every], label_send, label_recv.at[0], mate
    ).wait_send()


def multiply(a_ref, b_ref, o_hbm, o_ref, sem):
    rows = a_ref.shape[0]
    step = min(64, rows)
    copies = []
    for i in range(rows // step):
        part = pl.ds(i * step, step)
        o_ref[part, :] = jnp.dot(a_ref[part, :], b_ref[...], preferred_element_type=jnp.float32)
        copies.append(pltpu.make_async_copy(o_ref.at[part], o_hbm.at[part], sem.at[i]))
        copies[-1].start()
    for copy in copies:
        copy.wait()


def pinned(operand):
    return pltpu.with_memory_space_constraint(operand, pltpu.HBM)


def shards(x_count, y_count, amplitudes, integrals, in_tile, counts, out_tile, owner_map):
    slot_count, piece, width = integrals.shape
    row_count, deep = amplitudes.shape
    tile_total = owner_map.shape[0]
    wide_count = lax.axis_size("wide")
    narrow_count = lax.axis_size("narrow")
    tile_count = deep // (piece * narrow_count)
    own_count = tile_total // wide_count
    wide_out = own_count * width
    vmem = pltpu.VMEM
    dma = pltpu.SemaphoreType.DMA
    bf16, f32, i32 = jnp.bfloat16, jnp.float32, jnp.int32
    hbm = pl.BlockSpec(memory_space=pl.ANY)
    whole = pl.BlockSpec(memory_space=pltpu.VMEM)
    full = pl.pallas_call(
        functools.partial(exchange, (x_count, y_count, own_count, tile_count)),
        out_shape=jax.ShapeDtypeStruct((tile_count, narrow_count, piece, wide_out), bf16),
        in_specs=[hbm, hbm, pl.BlockSpec(memory_space=pltpu.SMEM), hbm, hbm],
        out_specs=hbm,
        cost_estimate=pl.CostEstimate(flops=10**9, bytes_accessed=10**8, transcendentals=0),
        scratch_shapes=[
            vmem((slot_count, piece, width), bf16),
            vmem((1, slot_count), i32),
            vmem((1, slot_count), i32),
            vmem((1, tile_total), i32),
            vmem((1, wide_count), i32),
            pltpu.SMEM((1, wide_count), i32),
            vmem((wide_count, piece, width), bf16),
            vmem((wide_count, 1, width), f32),
            vmem((wide_count, piece, width), bf16),
            vmem((wide_count, 1, width), f32),
            vmem((tile_count, piece, wide_out), bf16),
            dma((4,)),
            dma(()),
            dma((2,)),
            dma(()),
            dma((2,)),
            dma(()),
            dma((2,)),
            dma((2,)),
            dma(()),
            pltpu.SemaphoreType.REGULAR((narrow_count,)),
        ],
        compiler_params=pltpu.CompilerParams(
            collective_id=0, has_side_effects=True, vmem_limit_bytes=8 << 20
        ),
    )(
        pinned(integrals),
        pinned(in_tile.reshape(1, slot_count)),
        counts,
        pinned(out_tile.reshape(1, slot_count)),
        pinned(owner_map.reshape(1, tile_total)),
    )
    full = full.reshape(deep, wide_out)
    return pl.pallas_call(
        multiply,
        out_shape=jax.ShapeDtypeStruct((row_count, wide_out), f32),
        in_specs=[whole, whole],
        out_specs=hbm,
        scratch_shapes=[vmem((row_count, wide_out), f32), dma((8,))],
        compiler_params=pltpu.CompilerParams(vmem_limit_bytes=8 << 20),
    )(amplitudes, full)


def solution(mesh):
    wide_count = mesh.shape["wide"]
    y_count = 8 if wide_count == 64 else max(1, wide_count // 4)
    x_count = wide_count // (CORES * y_count)
    return jax.shard_map(
        functools.partial(shards, x_count, y_count),
        mesh=mesh,
        in_specs=(
            P("narrow", None),
            P("wide", "narrow", None),
            P("wide"),
            P("wide"),
            P("wide"),
            P(),
        ),
        out_specs=P("narrow", "wide"),
        check_vma=False,
    )
```
